32 devices in a mesh: lon: 2 (over x), lat: 4 (over z), tm: 4 (over y, core).
Axes of the slice: x: 2, y: 2, z: 4, core: 2. Of those that a mesh axis runs over, the one named last changes fastest.
Arguments:
- precip: float32 [128, 1024, 256], P('tm', 'lat', 'lon'), may hold values from 0.02 to 8
- offset: float32 [128, 1024, 256], P('tm', 'lat', 'lon'), may hold values from -3 to 3
- coefficients: float32 [32, 256, 64], P('tm', 'lat', 'lon'), may hold values from -2 to 2
- inverse_diag: float32 [32, 256, 64], P('tm', 'lat', 'lon'), may hold values from 0.02 to 0.2
Outputs:
- newton_step: float32 [32, 256, 64], P('tm', 'lat', 'lon')
- residual: float32 [32, 256, 64], P('tm', 'lat', 'lon')
The draws below stay inside these ranges and needn't reach their ends.
All inputs are finite; a program needn't handle non-finite values.
Results may differ from the reference program's by a relative error of at most 0.0003.
Values sent between devices are 32-bit elements; how exact they have to be, the bound alone decides.
A program may use at most 64 MiB of HBM per device.

```python
import math
import jax
import jax.numpy as jnp
from jax import lax

NT = 128
NLAT = 1024
NLON = 256
KT = 32
KLAT = 256
KLON = 64


def shard_levels(own_key, shape, split, low, top_value):
    level = 1.0
    for axis_at, shards_of in split:
        heights = jax.random.uniform(jax.random.fold_in(jax.random.fold_in(own_key, 6), axis_at), (shards_of,), jnp.float32, low / len(split), top_value / len(split))
        level = level * jnp.repeat(jnp.exp(heights), shape[axis_at] // shards_of).reshape((-1,) + (1,) * (len(shape) - 1 - axis_at))
    return level


def normal_values(stream_key, shape, deviation, limit, pieces=(), held_as=jnp.bfloat16):
    drawn = deviation * jax.random.normal(stream_key, shape, jnp.float32)
    if pieces:
        drawn = drawn * shard_levels(stream_key, shape, pieces, -0.22, 0.18)
    return jnp.clip(drawn, -limit, limit).astype(held_as)


def setup_inputs(seed: int = 0) -> dict:
    keys = jax.random.split(jax.random.key(seed), 5)
    precip = jnp.clip(jnp.exp(math.log(8.0) - 5.9914646 * jax.random.uniform(keys[0], (NT, NLAT, NLON), jnp.float32) ** shard_levels(keys[0], (NT, NLAT, NLON), ((0, 4), (1, 4), (2, 2)), -0.2, 0.2)), 0.02, 8.0)
    offset = normal_values(keys[1], (NT, NLAT, NLON), 0.5, 3.0, ((0, 4), (1, 4), (2, 2)), jnp.float32)
    coefficients = normal_values(keys[2], (KT, KLAT, KLON), 0.3, 2.0, ((0, 4), (1, 4), (2, 2)), jnp.float32)
    inverse_diag = jnp.clip(jnp.exp(math.log(0.2) - 2.3025851 * jax.random.uniform(keys[3], (KT, KLAT, KLON), jnp.float32) ** shard_levels(keys[3], (KT, KLAT, KLON), ((0, 4), (1, 4), (2, 2)), -0.2, 0.2)), 0.02, 0.2)
    return dict(precip=precip, offset=offset, coefficients=coefficients, inverse_diag=inverse_diag)


tweedie_power = 1.6
smooth = 0.5
highest = lax.Precision.HIGHEST


def spline(offsets):
    distance = jnp.abs(offsets)
    near_part = (4.0 - 6.0 * distance * distance + 3.0 * distance * distance * distance) / 6.0
    far_part = jnp.maximum(2.0 - distance, 0.0) ** 3 / 6.0
    return jnp.where(distance < 1.0, near_part, far_part)


def spline_basis(cell_count, knot_count, cyclic):
    cell_pos = jnp.arange(cell_count, dtype=jnp.int32)[:, None]
    knot_pos = jnp.arange(knot_count, dtype=jnp.int32)[None, :]
    spread = cell_pos - 4 * knot_pos
    if cyclic:
        spread = jnp.mod(spread + cell_count // 2, cell_count) - cell_count // 2
        centred = spread.astype(jnp.float32) - 1.5
        return spline(centred / 4.0) + spline((centred - cell_count) / 4.0) + spline((centred + cell_count) / 4.0)
    return spline((spread.astype(jnp.float32) - 1.5) / 4.0)


def evaluate(vector, tables):
    time_tab, lat_tab, lon_tab = tables
    partial_value = jnp.einsum('tae,le->tal', vector, lon_tab, precision=highest)
    partial_value = jnp.einsum('tal,ba->tbl', partial_value, lat_tab, precision=highest)
    return jnp.einsum('tbl,st->sbl', partial_value, time_tab, precision=highest)


def adjoint(cell_values, tables):
    time_tab, lat_tab, lon_tab = tables
    partial_value = jnp.einsum('sbl,st->tbl', cell_values, time_tab, precision=highest)
    partial_value = jnp.einsum('tbl,ba->tal', partial_value, lat_tab, precision=highest)
    return jnp.einsum('tal,le->tae', partial_value, lon_tab, precision=highest)


def penalty(vector):
    summed = 18.0 * vector
    for along in (0, 1):
        padded = jnp.pad(vector, [(2, 2) if which == along else (0, 0) for which in range(3)])
        length = vector.shape[along]
        for first_at, factor in ((0, 1.0), (1, -4.0), (3, -4.0), (4, 1.0)):
            summed = summed + factor * lax.slice_in_dim(padded, first_at, first_at + length, axis=along)
    for moved, factor in ((2, 1.0), (1, -4.0), (-1, -4.0), (-2, 1.0)):
        summed = summed + factor * jnp.roll(vector, moved, axis=2)
    return smooth * summed


def reference(precip, offset, coefficients, inverse_diag):
    tables = (spline_basis(NT, KT, False), spline_basis(NLAT, KLAT, False), spline_basis(NLON, KLON, True))
    lat_index = jnp.arange(NLAT, dtype=jnp.float32)
    area_weight = jnp.cos((90.0 - (lat_index + 0.5) * 180.0 / NLAT) * (jnp.pi / 180.0))[None, :, None]
    linear = offset + evaluate(coefficients, tables)
    tilted = jnp.exp((1.0 - tweedie_power) * linear)
    mean_rate = jnp.exp(linear)
    weight = area_weight * mean_rate * tilted
    gradient = adjoint(area_weight * (mean_rate - precip) * tilted, tables) + penalty(coefficients)
    residual = -gradient
    scaled = inverse_diag * residual
    direction = scaled
    precond_norm = jnp.sum(residual * scaled)
    newton_step = jnp.zeros_like(coefficients)
    for sweep in range(2):
        image = adjoint(weight * evaluate(direction, tables), tables) + penalty(direction)
        step_size = precond_norm / jnp.sum(direction * image)
        newton_step = newton_step + step_size * direction
        residual = residual - step_size * image
        if sweep == 0:
            scaled = inverse_diag * residual
            next_norm = jnp.sum(residual * scaled)
            direction = scaled + (next_norm / precond_norm) * direction
            precond_norm = next_norm
    return newton_step, residual
```

```python
import functools

import numpy as np
import jax
import jax.numpy as jnp
from jax import lax
from jax.experimental import pallas as pl
from jax.experimental.pallas import tpu as pltpu
from jax.sharding import PartitionSpec as P

tweedie_power = 1.6
smooth = 0.5
bf16 = jnp.bfloat16
f32 = jnp.float32
LANES = 128
LEAD = 8
AXES = ("lon", "lat", "tm")


def spline(offsets):
    distance = np.abs(np.asarray(offsets, np.float64))
    near_part = (4.0 - 6.0 * distance**2 + 3.0 * distance**3) / 6.0
    far_part = np.maximum(2.0 - distance, 0.0) ** 3 / 6.0
    return np.where(distance < 1.0, near_part, far_part)


def halves(table):
    high = table.astype(np.float32).astype(bf16)
    low = (table - high.astype(np.float64)).astype(np.float32).astype(bf16)
    return high, low


def lat_tables(count):
    knots = np.arange(count + 2 * LEAD) - LEAD
    cells = np.arange(4 * count)
    high, low = halves(spline((cells[:, None] - 4.0 * knots[None, :] - 1.5) / 4.0))
    forward = np.concatenate([high, high, low], axis=1)
    back = np.concatenate([high.T, low.T], axis=0)
    return forward, back


def lon_tables(count):
    lanes = np.arange(LANES)
    knots = np.where(lanes >= LANES - 2, lanes - LANES, lanes)
    valid = knots < count + 2
    cells = np.arange(4 * count)
    table = spline((cells[:, None] - 4.0 * knots[None, :] - 1.5) / 4.0) * valid[None, :]
    high, low = halves(table)
    gap = count + 8
    forward = (
        high.T.astype(np.float32)
        + np.roll(high.T.astype(np.float32), gap, 0)
        + np.roll(low.T.astype(np.float32), 2 * gap, 0)
    ).astype(bf16)
    return forward, high, low


def area_table(lat_total):
    index = np.arange(lat_total, dtype=np.float32)
    degrees = np.float32(90.0) - (index + np.float32(0.5)) * np.float32(180.0) / np.float32(lat_total)
    values = np.cos((degrees * np.float32(np.pi / 180.0)).astype(np.float64)).astype(np.float32)
    return np.ascontiguousarray(np.broadcast_to(values[:, None], (lat_total, LANES)))


def time_taps():
    taps = []
    for phase in range(4):
        row = []
        for shift in range(-2, 3):
            weight = float(spline((phase - 4.0 * shift - 1.5) / 4.0))
            if weight != 0.0:
                row.append((shift + 2, weight))
        taps.append(row)
    return taps


def split(values):
    high = values.astype(bf16)
    return high, (values - high.astype(f32)).astype(bf16)


def kernel(
    counts,
    mesh_sizes,
    coef_ref,
    inv_ref,
    area_hbm,
    offset_hbm,
    precip_hbm,
    lon_fwd,
    lat_fwd,
    lat_back,
    lon_high,
    lon_low,
    step_ref,
    resid_ref,
    weight,
    precip,
    area,
    cells,
    coef,
    inv,
    res,
    dir0,
    dir1,
    img0,
    img1,
    lon_send,
    lon_recv,
    lat_send,
    lat_recv,
    tm_send,
    tm_recv,
    sum_lon,
    sum_lat,
    sum_tm,
    load_sem,
    lon_sems,
    lat_sems,
    tm_sems,
    sum_lon_sems,
    sum_lat_sems,
    sum_tm_sems,
):
    time_n, lat_n, lon_n = counts
    padded_time = time_n + 4
    rows = lat_n + 2 * LEAD
    half = LANES // 2
    own_t = slice(2, 2 + time_n)
    own_a = slice(LEAD, LEAD + lat_n)
    me = {name: lax.axis_index(name) for name in AXES}
    size = dict(zip(AXES, mesh_sizes))
    pending = []

    lat_cells = 4 * lat_n
    loads = [
        pltpu.make_async_copy(
            area_hbm.at[pl.ds(pl.multiple_of(me["lat"] * lat_cells, lat_cells), lat_cells)],
            area,
            load_sem.at[0],
        )
    ]
    part = 2 * time_n
    for i in range(2):
        span = pl.ds(i * part, part)
        loads.append(pltpu.make_async_copy(offset_hbm.at[span], weight.at[span], load_sem.at[1 + 2 * i]))
        loads.append(pltpu.make_async_copy(precip_hbm.at[span], precip.at[span], load_sem.at[2 + 2 * i]))
    for load in loads:
        load.start()

    barrier = pltpu.get_barrier_semaphore()
    for name in AXES:
        for hop in range(1, size[name]):
            pl.semaphore_signal(
                barrier,
                inc=1,
                device_id={name: lax.rem(me[name] + hop, size[name])},
                device_id_type=pl.DeviceIdType.MESH,
            )

    coef[...] = jnp.zeros(coef.shape, f32)
    inv[...] = jnp.zeros(inv.shape, f32)
    coef[own_t, own_a, 0:lon_n] = coef_ref[...]
    inv[own_t, own_a, 0:lon_n] = inv_ref[...]
    pl.semaphore_wait(barrier, sum(size[name] - 1 for name in AXES))

    lane = lax.broadcasted_iota(jnp.int32, (rows, LANES), 1)
    low_lanes = (lane < 2) | (lane >= LANES - 2)
    high_lanes = (lane >= lon_n - 2) & (lane < lon_n + 2)
    used_lanes = (lane < lon_n + 2) | (lane >= LANES - 2)
    own_lanes = lane[0:lat_n] < lon_n

    def remote(src, dst, sems, at, name, to):
        return pltpu.make_async_remote_copy(
            src_ref=src,
            dst_ref=dst,
            send_sem=sems.at[0, at],
            recv_sem=sems.at[1, at],
            device_id={name: to},
            device_id_type=pl.DeviceIdType.MESH,
        )

    def neighbours(name):
        count = size[name]
        return lax.rem(me[name] + count - 1, count), lax.rem(me[name] + 1, count)

    def exchange(pairs, hooks):
        copies = []
        before, after = neighbours("lon")
        for ref, bank in pairs:
            packed = jnp.zeros((rows, LANES), f32)
            for t in range(padded_time):
                slab = ref[t]
                at = 4 * t
                packed = jnp.where(
                    (lane >= at) & (lane < at + 4), pltpu.roll(slab, (at + 2) % LANES, 1), packed
                )
                at = half + 4 * t
                packed = jnp.where(
                    (lane >= at) & (lane < at + 4),
                    pltpu.roll(slab, (at - lon_n + 2) % LANES, 1),
                    packed,
                )
            full = jnp.concatenate([packed, jnp.zeros((LANES - rows, LANES), f32)], axis=0)
            lon_send[bank] = full.T
            low = pl.ds(0, 4 * padded_time)
            high = pl.ds(half, 4 * padded_time)
            down = remote(
                lon_send.at[bank, low], lon_recv.at[bank, high], lon_sems, 2 * bank, "lon", before
            )
            up = remote(
                lon_send.at[bank, high], lon_recv.at[bank, low], lon_sems, 2 * bank + 1, "lon", after
            )
            down.start()
            up.start()
            copies.append((down, up))
            pending.append((None, down))
            pending.append((None, up))
        hooks[0]()
        for (ref, bank), (down, up) in zip(pairs, copies):
            down.wait_recv()
            up.wait_recv()
            back = lon_recv[bank].T[0:rows]
            for t in range(padded_time):
                at = 4 * t
                mine = jnp.where(low_lanes, pltpu.roll(back, (LANES - at - 2) % LANES, 1), 0.0)
                at = half + 4 * t
                mine = jnp.where(high_lanes, pltpu.roll(back, (LANES - at + lon_n - 2) % LANES, 1), mine)
                ref[t] = ref[t] + mine

        def ends(name, send, recv, sems, load, store, hook):
            before, after = neighbours(name)
            has_low = me[name] > 0
            has_high = me[name] < size[name] - 1
            copies = []
            for ref, bank in pairs:
                load(ref, bank)
                down = remote(send.at[bank, 0], recv.at[bank, 1], sems, 2 * bank, name, before)
                up = remote(send.at[bank, 1], recv.at[bank, 0], sems, 2 * bank + 1, name, after)
                pl.when(has_low)(down.start)
                pl.when(has_high)(up.start)
                copies.append((down, up))
                pending.append((has_low, down))
                pending.append((has_high, up))
            hook()
            for (ref, bank), (down, up) in zip(pairs, copies):

                @pl.when(has_low)
                def _():
                    up.wait_recv()
                    store(ref, bank, 0)

                @pl.when(has_high)
                def _():
                    down.wait_recv()
                    store(ref, bank, 1)

        starts = (LEAD - 2, LEAD + lat_n - 2)

        def lat_load(ref, bank):
            for t in range(padded_time):
                for side, start in enumerate(starts):
                    lat_send[bank, side, 4 * t : 4 * t + 4] = ref[t, start : start + 4]

        def lat_store(ref, bank, side):
            start = starts[side]
            for t in range(padded_time):
                ref[t, start : start + 4] = (
                    ref[t, start : start + 4] + lat_recv[bank, side, 4 * t : 4 * t + 4]
                )

        ends("lat", lat_send, lat_recv, lat_sems, lat_load, lat_store, hooks[1])

        def tm_load(ref, bank):
            for side, start in enumerate((0, time_n)):
                for i in range(2):
                    tm_send[bank, side, i] = ref[start + 2 * i] + pltpu.roll(
                        ref[start + 2 * i + 1], half, 1
                    )

        def tm_store(ref, bank, side):
            start = (0, time_n)[side]
            for i in range(2):
                got = tm_recv[bank, side, i]
                ref[start + 2 * i] = ref[start + 2 * i] + jnp.where(used_lanes, got, 0.0)
                ref[start + 2 * i + 1] = ref[start + 2 * i + 1] + jnp.where(
                    used_lanes, pltpu.roll(got, half, 1), 0.0
                )

        ends("tm", tm_send, tm_recv, tm_sems, tm_load, tm_store, hooks[2])

    slots = {"lon": sum_lon, "lat": sum_lat, "tm": sum_tm}
    slot_sems = {"lon": sum_lon_sems, "lat": sum_lat_sems, "tm": sum_tm_sems}

    class Total:
        def __init__(self, bank, value):
            self.bank, self.value, self.stage = bank, value, 0
            self.send()

        def send(self):
            name = AXES[self.stage]
            count = size[name]
            buf = slots[name]
            buf[self.bank, me[name]] = self.value
            self.copies = []
            for hop in range(1, count):
                at = self.bank * count + hop
                mine = buf.at[self.bank, me[name]]
                out = remote(mine, mine, slot_sems[name], at, name, lax.rem(me[name] + hop, count))
                out.start()
                pending.append((None, out))
                theirs = buf.at[self.bank, lax.rem(me[name] + count - hop, count)]
                self.copies.append(
                    remote(theirs, theirs, slot_sems[name], at, name, lax.rem(me[name] + hop, count))
                )

        def advance(self):
            name = AXES[self.stage]
            for copy in self.copies:
                copy.wait_recv()
            value = slots[name][self.bank, 0]
            for i in range(1, size[name]):
                value = value + slots[name][self.bank, i]
            self.value = value
            self.stage += 1
            if self.stage < len(AXES):
                self.send()

        def read(self, first):
            tile = self.value[8 * first : 8 * first + 8]
            return jnp.sum(jnp.sum(tile, axis=0, keepdims=True), axis=1, keepdims=True)

    def tile_of(values):
        return jnp.sum(values.reshape(-1, 8, LANES), axis=0)

    def own_tile(left, right):
        masked = jnp.where(own_lanes[None], left[own_t, own_a] * right[own_t, own_a], 0.0)
        return tile_of(masked)

    taps = time_taps()

    def synth(z, m, phase):
        total = None
        for at, factor in taps[phase]:
            term = z[m + at] * factor
            total = term if total is None else total + term
        return total

    def columns(t):
        return slice(LANES * t, LANES * (t + 1))

    def apply(vec, image, cell_values, hooks):
        gap = lon_n + 8
        for pair in range(padded_time // 2):
            values = vec[2 * pair : 2 * pair + 2].reshape(2 * rows, LANES)
            high = values.astype(bf16).astype(f32)
            low = values - high
            stacked = (high + pltpu.roll(low, gap, 1) + pltpu.roll(high, 2 * gap, 1)).astype(bf16)
            wide = jnp.dot(stacked, lon_fwd[...], preferred_element_type=f32)
            high, low = split(jnp.concatenate([wide[0:rows], wide[rows:]], axis=1))
            stacked = jnp.concatenate([high, low, high], axis=0)
            cells[:, 2 * LANES * pair : 2 * LANES * (pair + 1)] = jnp.dot(
                lat_fwd[...], stacked, preferred_element_type=f32
            )
        hooks[0]()

        def group(g, carry):
            at = pl.ds(pl.multiple_of(g * 8, 8), 8)
            z = [cells[at, columns(t)] for t in range(padded_time)]
            sums = [None] * padded_time
            for m in range(time_n):
                for phase in range(4):
                    value = cell_values(4 * m + phase, at, synth(z, m, phase))
                    for shift, factor in taps[phase]:
                        term = value * factor
                        old = sums[m + shift]
                        sums[m + shift] = term if old is None else old + term
                cells[at, columns(m)] = sums[m]
            for t in range(time_n, padded_time):
                cells[at, columns(t)] = sums[t]
            return carry

        lax.fori_loop(0, lat_cells // 8, group, 0)
        hooks[1]()
        for pair in range(padded_time // 2):
            high, low = split(cells[:, 2 * LANES * pair : 2 * LANES * (pair + 1)])
            both = jnp.dot(lat_back[...], high, preferred_element_type=f32)
            rest = jnp.dot(lat_back[0:rows], low, preferred_element_type=f32)
            knots = both[0:rows] + both[rows:] + rest
            high, low = split(jnp.concatenate([knots[:, 0:LANES], knots[:, LANES:]], axis=0))
            out = (
                jnp.dot(high, lon_high[...], preferred_element_type=f32)
                + jnp.dot(low, lon_high[...], preferred_element_type=f32)
                + jnp.dot(high, lon_low[...], preferred_element_type=f32)
            )
            image[2 * pair] = out[0:rows]
            image[2 * pair + 1] = out[rows:]
        for t in range(2, 2 + time_n):
            mid = vec[t, own_a]
            outer = vec[t - 2, own_a] + vec[t + 2, own_a]
            inner = vec[t - 1, own_a] + vec[t + 1, own_a]
            outer = outer + vec[t, LEAD - 2 : LEAD + lat_n - 2] + vec[t, LEAD + 2 : LEAD + lat_n + 2]
            inner = inner + vec[t, LEAD - 1 : LEAD + lat_n - 1] + vec[t, LEAD + 1 : LEAD + lat_n + 1]
            outer = outer + pltpu.roll(mid, 2, 1) + pltpu.roll(mid, LANES - 2, 1)
            inner = inner + pltpu.roll(mid, 1, 1) + pltpu.roll(mid, LANES - 1, 1)
            bent = smooth * (18.0 * mid - 4.0 * inner + outer)
            image[t, own_a] = image[t, own_a] + jnp.where(own_lanes, bent, 0.0)
        hooks[2]()

    def nothing():
        pass

    idle = (nothing, nothing, nothing)

    def gradient_cells(s, at, value):
        linear = weight[s, at] + value
        scale = area[at]
        rate = scale * jnp.exp((2.0 - tweedie_power) * linear)
        tilted = scale * jnp.exp((1.0 - tweedie_power) * linear)
        weight[s, at] = rate
        return rate - precip[s, at] * tilted

    def weighted_cells(s, at, value):
        return weight[s, at] * value

    exchange(((coef, 0), (inv, 1)), idle)
    for load in loads:
        load.wait()
    apply(coef, img0, gradient_cells, idle)
    exchange(((img0, 2),), idle)
    res[...] = -img0[...]
    dir0[...] = inv[...] * res[...]
    first_norm = own_tile(res, dir0)

    apply(dir0, img0, weighted_cells, idle)
    sums = Total(0, jnp.concatenate([first_norm, tile_of(dir0[...] * img0[...])], axis=0))
    exchange(((img0, 3),), (sums.advance,) * 3)
    norm = sums.read(0)
    first_step = norm / sums.read(1)
    res[...] = res[...] - first_step[None] * img0[...]
    dir1[...] = inv[...] * res[...]
    tile = own_tile(res, dir1)
    sums = Total(1, jnp.concatenate([tile, jnp.zeros_like(tile)], axis=0))

    apply(dir1, img1, weighted_cells, (sums.advance,) * 3)
    next_norm = sums.read(0)
    beta = next_norm / norm
    dir1[...] = dir1[...] + beta[None] * dir0[...]
    tile = tile_of(dir1[...] * img1[...]) + beta * own_tile(dir1, img0)
    sums = Total(2, jnp.concatenate([tile, jnp.zeros_like(tile)], axis=0))
    exchange(((img1, 4),), (sums.advance,) * 3)
    second_step = next_norm / sums.read(0)
    for t in range(time_n):
        at = (t + 2, own_a)
        step = first_step * dir0[at] + second_step * dir1[at]
        left = res[at] - second_step * (img1[at] + beta * img0[at])
        step_ref[t] = step[:, 0:lon_n]
        resid_ref[t] = left[:, 0:lon_n]
    for condition, copy in pending:
        if condition is None:
            copy.wait_send()
        else:
            pl.when(condition)(copy.wait_send)


def solution(mesh):
    mesh_sizes = tuple(mesh.shape[name] for name in AXES)

    def per_device(precip, offset, coefficients, inverse_diag):
        time_n, lat_n, lon_n = coefficients.shape
        hours, lat_cells, lon_cells = precip.shape
        assert lon_cells == LANES and 3 * (lon_n + 8) <= LANES and 8 * (time_n + 4) <= LANES
        rows = lat_n + 2 * LEAD
        padded_time = time_n + 4
        lat_fwd, lat_back = lat_tables(lat_n)
        lon_fwd, lon_high, lon_low = lon_tables(lon_n)
        knots = pltpu.VMEM((padded_time, rows, LANES), f32)
        n_lon, n_lat, n_tm = mesh_sizes
        banks, totals = 5, 3
        vmem = pl.BlockSpec(memory_space=pltpu.VMEM)
        hbm = pl.BlockSpec(memory_space=pl.ANY)
        shape = jax.ShapeDtypeStruct(coefficients.shape, f32)
        dma = pltpu.SemaphoreType.DMA
        return pl.pallas_call(
            functools.partial(kernel, (time_n, lat_n, lon_n), mesh_sizes),
            out_shape=(shape, shape),
            in_specs=[vmem, vmem, hbm, hbm, hbm] + [vmem] * 5,
            out_specs=(vmem, vmem),
            scratch_shapes=[
                pltpu.VMEM((hours, lat_cells, lon_cells), f32),
                pltpu.VMEM((hours, lat_cells, lon_cells), f32),
                pltpu.VMEM((lat_cells, LANES), f32),
                pltpu.VMEM((lat_cells, padded_time * LANES), f32),
            ]
            + [knots] * 7
            + [
                pltpu.VMEM((banks, LANES, LANES), f32),
                pltpu.VMEM((banks, LANES, LANES), f32),
                pltpu.VMEM((banks, 2, 4 * padded_time, LANES), f32),
                pltpu.VMEM((banks, 2, 4 * padded_time, LANES), f32),
                pltpu.VMEM((banks, 2, 2, rows, LANES), f32),
                pltpu.VMEM((banks, 2, 2, rows, LANES), f32),
                pltpu.VMEM((totals, n_lon, 16, LANES), f32),
                pltpu.VMEM((totals, n_lat, 16, LANES), f32),
                pltpu.VMEM((totals, n_tm, 16, LANES), f32),
                dma((5,)),
                dma((2, 2 * banks)),
                dma((2, 2 * banks)),
                dma((2, 2 * banks)),
                dma((2, totals * n_lon)),
                dma((2, totals * n_lat)),
                dma((2, totals * n_tm)),
            ],
            compiler_params=pltpu.CompilerParams(
                collective_id=0, has_side_effects=True, vmem_limit_bytes=60 * 1024 * 1024
            ),
        )(
            coefficients,
            inverse_diag,
            jnp.asarray(area_table(lat_cells * n_lat)),
            offset,
            precip,
            jnp.asarray(lon_fwd),
            jnp.asarray(lat_fwd),
            jnp.asarray(lat_back),
            jnp.asarray(lon_high),
            jnp.asarray(lon_low),
        )

    spec = P("tm", "lat", "lon")
    return jax.shard_map(
        per_device,
        mesh=mesh,
        in_specs=(spec,) * 4,
        out_specs=(spec,) * 2,
        check_vma=False,
    )
```

```python
import functools

import numpy as np
import jax
import jax.numpy as jnp
from jax import lax
from jax.experimental import pallas as pl
from jax.experimental.pallas import tpu as pltpu
from jax.sharding import PartitionSpec as P

tweedie_power = 1.6
smooth = 0.5
bf16 = jnp.bfloat16
f32 = jnp.float32
LANES = 128
LEAD = 8
AXES = ("lon", "lat", "tm")


def spline(offsets):
    distance = np.abs(np.asarray(offsets, np.float64))
    near_part = (4.0 - 6.0 * distance**2 + 3.0 * distance**3) / 6.0
    far_part = np.maximum(2.0 - distance, 0.0) ** 3 / 6.0
    return np.where(distance < 1.0, near_part, far_part)


def halves(table):
    high = table.astype(np.float32).astype(bf16)
    low = (table - high.astype(np.float64)).astype(np.float32).astype(bf16)
    return high, low


def lat_tables(count):
    knots = np.arange(count + 2 * LEAD) - LEAD
    cells = np.arange(4 * count)
    high, low = halves(spline((cells[:, None] - 4.0 * knots[None, :] - 1.5) / 4.0))
    forward = np.concatenate([high, high, low], axis=1)
    back = np.concatenate([high.T, low.T], axis=0)
    return forward, back


def lon_tables(count):
    lanes = np.arange(LANES)
    knots = np.where(lanes >= LANES - 2, lanes - LANES, lanes)
    valid = knots < count + 2
    cells = np.arange(4 * count)
    table = spline((cells[:, None] - 4.0 * knots[None, :] - 1.5) / 4.0) * valid[None, :]
    high, low = halves(table)
    gap = count + 8
    forward = (
        high.T.astype(np.float32)
        + np.roll(high.T.astype(np.float32), gap, 0)
        + np.roll(low.T.astype(np.float32), 2 * gap, 0)
    ).astype(bf16)
    return forward, high, low


def area_table(lat_total):
    index = np.arange(lat_total, dtype=np.float32)
    degrees = np.float32(90.0) - (index + np.float32(0.5)) * np.float32(180.0) / np.float32(lat_total)
    values = np.cos((degrees * np.float32(np.pi / 180.0)).astype(np.float64)).astype(np.float32)
    return np.ascontiguousarray(np.broadcast_to(values[:, None], (lat_total, LANES)))


def time_taps():
    taps = []
    for phase in range(4):
        row = []
        for shift in range(-2, 3):
            weight = float(spline((phase - 4.0 * shift - 1.5) / 4.0))
            if weight != 0.0:
                row.append((shift + 2, weight))
        taps.append(row)
    return taps


def split(values):
    high = values.astype(bf16)
    return high, (values - high.astype(f32)).astype(bf16)


def kernel(
    counts,
    mesh_sizes,
    coef_ref,
    inv_ref,
    area_hbm,
    offset_hbm,
    precip_hbm,
    lon_fwd,
    lat_fwd,
    lat_back,
    lon_high,
    lon_low,
    step_ref,
    resid_ref,
    weight,
    precip,
    area,
    cells,
    coef,
    inv,
    res,
    dir0,
    dir1,
    img0,
    img1,
    lon_send,
    lon_recv,
    lat_send,
    lat_recv,
    tm_send,
    tm_recv,
    sum_lon,
    sum_lat,
    sum_tm,
    load_sem,
    lon_sems,
    lat_sems,
    tm_sems,
    sum_lon_sems,
    sum_lat_sems,
    sum_tm_sems,
):
    time_n, lat_n, lon_n = counts
    padded_time = time_n + 4
    rows = lat_n + 2 * LEAD
    half = LANES // 2
    own_t = slice(2, 2 + time_n)
    own_a = slice(LEAD, LEAD + lat_n)
    me = {name: lax.axis_index(name) for name in AXES}
    size = dict(zip(AXES, mesh_sizes))
    pending = []

    lat_cells = 4 * lat_n
    loads = [
        pltpu.make_async_copy(
            area_hbm.at[pl.ds(pl.multiple_of(me["lat"] * lat_cells, lat_cells), lat_cells)],
            area,
            load_sem.at[0],
        )
    ]
    part = 2 * time_n
    for i in range(2):
        span = pl.ds(i * part, part)
        loads.append(pltpu.make_async_copy(offset_hbm.at[span], weight.at[span], load_sem.at[1 + 2 * i]))
        loads.append(pltpu.make_async_copy(precip_hbm.at[span], precip.at[span], load_sem.at[2 + 2 * i]))
    for load in loads:
        load.start()

    barrier = pltpu.get_barrier_semaphore()
    for name in AXES:
        for hop in range(1, size[name]):
            pl.semaphore_signal(
                barrier,
                inc=1,
                device_id={name: lax.rem(me[name] + hop, size[name])},
                device_id_type=pl.DeviceIdType.MESH,
            )

    coef[...] = jnp.zeros(coef.shape, f32)
    inv[...] = jnp.zeros(inv.shape, f32)
    lane = lax.broadcasted_iota(jnp.int32, (rows, LANES), 1)
    low_lanes = (lane < 2) | (lane >= LANES - 2)
    high_lanes = (lane >= lon_n - 2) & (lane < lon_n + 2)
    used_lanes = (lane < lon_n + 2) | (lane >= LANES - 2)
    own_lanes = lane[0:lat_n] < lon_n
    batch = LANES // lon_n

    for source, held in ((coef_ref, coef), (inv_ref, inv)):
        for first in range(0, time_n, batch):
            block = source[first : first + batch].reshape(LANES, lat_n)
            if lat_n < LANES:
                block = jnp.concatenate([block, jnp.zeros((LANES, LANES - lat_n), f32)], axis=1)
            turned = block.T[0:lat_n]
            for i in range(batch):
                slab = pltpu.roll(turned, LANES - lon_n * i, 1) if i else turned
                held[2 + first + i, own_a] = jnp.where(own_lanes, slab, 0.0)
    pl.semaphore_wait(barrier, sum(size[name] - 1 for name in AXES))

    def remote(src, dst, sems, at, name, to):
        return pltpu.make_async_remote_copy(
            src_ref=src,
            dst_ref=dst,
            send_sem=sems.at[0, at],
            recv_sem=sems.at[1, at],
            device_id={name: to},
            device_id_type=pl.DeviceIdType.MESH,
        )

    def neighbours(name):
        count = size[name]
        return lax.rem(me[name] + count - 1, count), lax.rem(me[name] + 1, count)

    def exchange(pairs, hooks):
        copies = []
        before, after = neighbours("lon")
        for ref, bank in pairs:
            packed = jnp.zeros((rows, LANES), f32)
            for t in range(padded_time):
                slab = ref[t]
                at = 4 * t
                packed = jnp.where(
                    (lane >= at) & (lane < at + 4), pltpu.roll(slab, (at + 2) % LANES, 1), packed
                )
                at = half + 4 * t
                packed = jnp.where(
                    (lane >= at) & (lane < at + 4),
                    pltpu.roll(slab, (at - lon_n + 2) % LANES, 1),
                    packed,
                )
            full = jnp.concatenate([packed, jnp.zeros((LANES - rows, LANES), f32)], axis=0)
            lon_send[bank] = full.T
            low = pl.ds(0, 4 * padded_time)
            high = pl.ds(half, 4 * padded_time)
            down = remote(
                lon_send.at[bank, low], lon_recv.at[bank, high], lon_sems, 2 * bank, "lon", before
            )
            up = remote(
                lon_send.at[bank, high], lon_recv.at[bank, low], lon_sems, 2 * bank + 1, "lon", after
            )
            down.start()
            up.start()
            copies.append((down, up))
            pending.append((None, down))
            pending.append((None, up))
        hooks[0]()
        for (ref, bank), (down, up) in zip(pairs, copies):
            down.wait_recv()
            up.wait_recv()
            back = lon_recv[bank].T[0:rows]
            for t in range(padded_time):
                at = 4 * t
                mine = jnp.where(low_lanes, pltpu.roll(back, (LANES - at - 2) % LANES, 1), 0.0)
                at = half + 4 * t
                mine = jnp.where(high_lanes, pltpu.roll(back, (LANES - at + lon_n - 2) % LANES, 1), mine)
                ref[t] = ref[t] + mine

        def ends(name, send, recv, sems, load, store, hook):
            before, after = neighbours(name)
            has_low = me[name] > 0
            has_high = me[name] < size[name] - 1
            copies = []
            for ref, bank in pairs:
                load(ref, bank)
                down = remote(send.at[bank, 0], recv.at[bank, 1], sems, 2 * bank, name, before)
                up = remote(send.at[bank, 1], recv.at[bank, 0], sems, 2 * bank + 1, name, after)
                pl.when(has_low)(down.start)
                pl.when(has_high)(up.start)
                copies.append((down, up))
                pending.append((has_low, down))
                pending.append((has_high, up))
            hook()
            for (ref, bank), (down, up) in zip(pairs, copies):

                @pl.when(has_low)
                def _():
                    up.wait_recv()
                    store(ref, bank, 0)

                @pl.when(has_high)
                def _():
                    down.wait_recv()
                    store(ref, bank, 1)

        starts = (LEAD - 2, LEAD + lat_n - 2)

        def lat_load(ref, bank):
            for t in range(padded_time):
                for side, start in enumerate(starts):
                    lat_send[bank, side, 4 * t : 4 * t + 4] = ref[t, start : start + 4]

        def lat_store(ref, bank, side):
            start = starts[side]
            for t in range(padded_time):
                ref[t, start : start + 4] = (
                    ref[t, start : start + 4] + lat_recv[bank, side, 4 * t : 4 * t + 4]
                )

        ends("lat", lat_send, lat_recv, lat_sems, lat_load, lat_store, hooks[1])

        def tm_load(ref, bank):
            for side, start in enumerate((0, time_n)):
                for i in range(2):
                    tm_send[bank, side, i] = ref[start + 2 * i] + pltpu.roll(
                        ref[start + 2 * i + 1], half, 1
                    )

        def tm_store(ref, bank, side):
            start = (0, time_n)[side]
            for i in range(2):
                got = tm_recv[bank, side, i]
                ref[start + 2 * i] = ref[start + 2 * i] + jnp.where(used_lanes, got, 0.0)
                ref[start + 2 * i + 1] = ref[start + 2 * i + 1] + jnp.where(
                    used_lanes, pltpu.roll(got, half, 1), 0.0
                )

        ends("tm", tm_send, tm_recv, tm_sems, tm_load, tm_store, hooks[2])

    slots = {"lon": sum_lon, "lat": sum_lat, "tm": sum_tm}
    slot_sems = {"lon": sum_lon_sems, "lat": sum_lat_sems, "tm": sum_tm_sems}

    class Total:
        def __init__(self, bank, value):
            self.bank, self.value, self.stage = bank, value, 0
            self.send()

        def send(self):
            name = AXES[self.stage]
            count = size[name]
            buf = slots[name]
            buf[self.bank, me[name]] = self.value
            self.copies = []
            for hop in range(1, count):
                at = self.bank * count + hop
                mine = buf.at[self.bank, me[name]]
                out = remote(mine, mine, slot_sems[name], at, name, lax.rem(me[name] + hop, count))
                out.start()
                pending.append((None, out))
                theirs = buf.at[self.bank, lax.rem(me[name] + count - hop, count)]
                self.copies.append(
                    remote(theirs, theirs, slot_sems[name], at, name, lax.rem(me[name] + hop, count))
                )

        def advance(self):
            name = AXES[self.stage]
            for copy in self.copies:
                copy.wait_recv()
            value = slots[name][self.bank, 0]
            for i in range(1, size[name]):
                value = value + slots[name][self.bank, i]
            self.value = value
            self.stage += 1
            if self.stage < len(AXES):
                self.send()

        def read(self, first):
            tile = self.value[8 * first : 8 * first + 8]
            return jnp.sum(jnp.sum(tile, axis=0, keepdims=True), axis=1, keepdims=True)

    def tile_of(values):
        return jnp.sum(values.reshape(-1, 8, LANES), axis=0)

    def own_tile(left, right):
        masked = jnp.where(own_lanes[None], left[own_t, own_a] * right[own_t, own_a], 0.0)
        return tile_of(masked)

    taps = time_taps()

    def synth(z, m, phase):
        total = None
        for at, factor in taps[phase]:
            term = z[m + at] * factor
            total = term if total is None else total + term
        return total

    def columns(t):
        return slice(LANES * t, LANES * (t + 1))

    def apply(vec, image, cell_values, hooks):
        gap = lon_n + 8
        for pair in range(padded_time // 2):
            values = vec[2 * pair : 2 * pair + 2].reshape(2 * rows, LANES)
            high = values.astype(bf16).astype(f32)
            low = values - high
            stacked = (high + pltpu.roll(low, gap, 1) + pltpu.roll(high, 2 * gap, 1)).astype(bf16)
            wide = jnp.dot(stacked, lon_fwd[...], preferred_element_type=f32)
            high, low = split(jnp.concatenate([wide[0:rows], wide[rows:]], axis=1))
            stacked = jnp.concatenate([high, low, high], axis=0)
            cells[:, 2 * LANES * pair : 2 * LANES * (pair + 1)] = jnp.dot(
                lat_fwd[...], stacked, preferred_element_type=f32
            )
        hooks[0]()

        def group(g, carry):
            at = pl.ds(pl.multiple_of(g * 8, 8), 8)
            z = [cells[at, columns(t)] for t in range(padded_time)]
            sums = [None] * padded_time
            for m in range(time_n):
                for phase in range(4):
                    value = cell_values(4 * m + phase, at, synth(z, m, phase))
                    for shift, factor in taps[phase]:
                        term = value * factor
                        old = sums[m + shift]
                        sums[m + shift] = term if old is None else old + term
                cells[at, columns(m)] = sums[m]
            for t in range(time_n, padded_time):
                cells[at, columns(t)] = sums[t]
            return carry

        lax.fori_loop(0, lat_cells // 8, group, 0)
        hooks[1]()
        for pair in range(padded_time // 2):
            high, low = split(cells[:, 2 * LANES * pair : 2 * LANES * (pair + 1)])
            both = jnp.dot(lat_back[...], high, preferred_element_type=f32)
            rest = jnp.dot(lat_back[0:rows], low, preferred_element_type=f32)
            knots = both[0:rows] + both[rows:] + rest
            high, low = split(jnp.concatenate([knots[:, 0:LANES], knots[:, LANES:]], axis=0))
            out = (
                jnp.dot(high, lon_high[...], preferred_element_type=f32)
                + jnp.dot(low, lon_high[...], preferred_element_type=f32)
                + jnp.dot(high, lon_low[...], preferred_element_type=f32)
            )
            image[2 * pair] = out[0:rows]
            image[2 * pair + 1] = out[rows:]
        for t in range(2, 2 + time_n):
            mid = vec[t, own_a]
            outer = vec[t - 2, own_a] + vec[t + 2, own_a]
            inner = vec[t - 1, own_a] + vec[t + 1, own_a]
            outer = outer + vec[t, LEAD - 2 : LEAD + lat_n - 2] + vec[t, LEAD + 2 : LEAD + lat_n + 2]
            inner = inner + vec[t, LEAD - 1 : LEAD + lat_n - 1] + vec[t, LEAD + 1 : LEAD + lat_n + 1]
            outer = outer + pltpu.roll(mid, 2, 1) + pltpu.roll(mid, LANES - 2, 1)
            inner = inner + pltpu.roll(mid, 1, 1) + pltpu.roll(mid, LANES - 1, 1)
            bent = smooth * (18.0 * mid - 4.0 * inner + outer)
            image[t, own_a] = image[t, own_a] + jnp.where(own_lanes, bent, 0.0)
        hooks[2]()

    def nothing():
        pass

    idle = (nothing, nothing, nothing)

    def gradient_cells(s, at, value):
        linear = weight[s, at] + value
        scale = area[at]
        rate = scale * jnp.exp((2.0 - tweedie_power) * linear)
        tilted = scale * jnp.exp((1.0 - tweedie_power) * linear)
        weight[s, at] = rate
        return rate - precip[s, at] * tilted

    def weighted_cells(s, at, value):
        return weight[s, at] * value

    exchange(((coef, 0), (inv, 1)), idle)
    for load in loads:
        load.wait()
    apply(coef, img0, gradient_cells, idle)
    exchange(((img0, 2),), idle)
    res[...] = -img0[...]
    dir0[...] = inv[...] * res[...]
    first_norm = own_tile(res, dir0)

    apply(dir0, img0, weighted_cells, idle)
    sums = Total(0, jnp.concatenate([first_norm, tile_of(dir0[...] * img0[...])], axis=0))
    exchange(((img0, 3),), (sums.advance,) * 3)
    norm = sums.read(0)
    first_step = norm / sums.read(1)
    res[...] = res[...] - first_step[None] * img0[...]
    dir1[...] = inv[...] * res[...]
    tile = own_tile(res, dir1)
    sums = Total(1, jnp.concatenate([tile, jnp.zeros_like(tile)], axis=0))

    apply(dir1, img1, weighted_cells, (sums.advance,) * 3)
    next_norm = sums.read(0)
    beta = next_norm / norm
    dir1[...] = dir1[...] + beta[None] * dir0[...]
    tile = tile_of(dir1[...] * img1[...]) + beta * own_tile(dir1, img0)
    sums = Total(2, jnp.concatenate([tile, jnp.zeros_like(tile)], axis=0))
    exchange(((img1, 4),), (sums.advance,) * 3)
    second_step = next_norm / sums.read(0)
    for first in range(0, time_n, batch):
        packed = [None, None]
        for i in range(batch):
            at = (first + i + 2, own_a)
            step = first_step * dir0[at] + second_step * dir1[at]
            left = res[at] - second_step * (img1[at] + beta * img0[at])
            for which, value in enumerate((step, left)):
                slab = jnp.where(own_lanes, value, 0.0)
                slab = pltpu.roll(slab, lon_n * i, 1) if i else slab
                packed[which] = slab if i == 0 else packed[which] + slab
        for ref, value in zip((step_ref, resid_ref), packed):
            if lat_n < LANES:
                value = jnp.concatenate([value, jnp.zeros((LANES - lat_n, LANES), f32)], axis=0)
            ref[first : first + batch] = value.T[:, 0:lat_n].reshape(batch, lon_n, lat_n)
    for condition, copy in pending:
        if condition is None:
            copy.wait_send()
        else:
            pl.when(condition)(copy.wait_send)


def solution(mesh):
    mesh_sizes = tuple(mesh.shape[name] for name in AXES)

    def per_device(precip, offset, coefficients, inverse_diag):
        time_n, lat_n, lon_n = coefficients.shape
        hours, lat_cells, lon_cells = precip.shape
        assert lon_cells == LANES and 3 * (lon_n + 8) <= LANES and 8 * (time_n + 4) <= LANES
        assert LANES % lon_n == 0 and time_n % (LANES // lon_n) == 0 and lat_n <= LANES
        rows = lat_n + 2 * LEAD
        padded_time = time_n + 4
        lat_fwd, lat_back = lat_tables(lat_n)
        lon_fwd, lon_high, lon_low = lon_tables(lon_n)
        knots = pltpu.VMEM((padded_time, rows, LANES), f32)
        n_lon, n_lat, n_tm = mesh_sizes
        banks, totals = 5, 3
        vmem = pl.BlockSpec(memory_space=pltpu.VMEM)
        hbm = pl.BlockSpec(memory_space=pl.ANY)
        shape = jax.ShapeDtypeStruct((time_n, lon_n, lat_n), f32)
        dma = pltpu.SemaphoreType.DMA
        step, left = pl.pallas_call(
            functools.partial(kernel, (time_n, lat_n, lon_n), mesh_sizes),
            out_shape=(shape, shape),
            in_specs=[vmem, vmem, hbm, hbm, hbm] + [vmem] * 5,
            out_specs=(vmem, vmem),
            scratch_shapes=[
                pltpu.VMEM((hours, lat_cells, lon_cells), f32),
                pltpu.VMEM((hours, lat_cells, lon_cells), f32),
                pltpu.VMEM((lat_cells, LANES), f32),
                pltpu.VMEM((lat_cells, padded_time * LANES), f32),
            ]
            + [knots] * 7
            + [
                pltpu.VMEM((banks, LANES, LANES), f32),
                pltpu.VMEM((banks, LANES, LANES), f32),
                pltpu.VMEM((banks, 2, 4 * padded_time, LANES), f32),
                pltpu.VMEM((banks, 2, 4 * padded_time, LANES), f32),
                pltpu.VMEM((banks, 2, 2, rows, LANES), f32),
                pltpu.VMEM((banks, 2, 2, rows, LANES), f32),
                pltpu.VMEM((totals, n_lon, 16, LANES), f32),
                pltpu.VMEM((totals, n_lat, 16, LANES), f32),
                pltpu.VMEM((totals, n_tm, 16, LANES), f32),
                dma((5,)),
                dma((2, 2 * banks)),
                dma((2, 2 * banks)),
                dma((2, 2 * banks)),
                dma((2, totals * n_lon)),
                dma((2, totals * n_lat)),
                dma((2, totals * n_tm)),
            ],
            compiler_params=pltpu.CompilerParams(
                collective_id=0, has_side_effects=True, vmem_limit_bytes=60 * 1024 * 1024
            ),
        )(
            jnp.swapaxes(coefficients, 1, 2),
            jnp.swapaxes(inverse_diag, 1, 2),
            jnp.asarray(area_table(lat_cells * n_lat)),
            offset,
            precip,
            jnp.asarray(lon_fwd),
            jnp.asarray(lat_fwd),
            jnp.asarray(lat_back),
            jnp.asarray(lon_high),
            jnp.asarray(lon_low),
        )
        return jnp.swapaxes(step, 1, 2), jnp.swapaxes(left, 1, 2)

    spec = P("tm", "lat", "lon")
    return jax.shard_map(
        per_device,
        mesh=mesh,
        in_specs=(spec,) * 4,
        out_specs=(spec,) * 2,
        check_vma=False,
    )
```

```python
import functools

import numpy as np
import jax
import jax.numpy as jnp
from jax import lax
from jax.experimental import pallas as pl
from jax.experimental.pallas import tpu as pltpu
from jax.sharding import PartitionSpec as P

tweedie_power = 1.6
smooth = 0.5
bf16 = jnp.bfloat16
f32 = jnp.float32
LANES = 128
LEAD = 8
AXES = ("lon", "lat", "tm")


def spline(offsets):
    distance = np.abs(np.asarray(offsets, np.float64))
    near_part = (4.0 - 6.0 * distance**2 + 3.0 * distance**3) / 6.0
    far_part = np.maximum(2.0 - distance, 0.0) ** 3 / 6.0
    return np.where(distance < 1.0, near_part, far_part)


def halves(table):
    high = table.astype(np.float32).astype(bf16)
    low = (table - high.astype(np.float64)).astype(np.float32).astype(bf16)
    return high, low


def lat_tables(count):
    knots = np.arange(count + 2 * LEAD) - LEAD
    cells = np.arange(4 * count)
    high, low = halves(spline((cells[:, None] - 4.0 * knots[None, :] - 1.5) / 4.0))
    forward = np.concatenate([high, high, low], axis=1)
    back = np.concatenate([high.T, low.T], axis=0)
    return forward, back


def lon_tables(count):
    lanes = np.arange(LANES)
    knots = np.where(lanes >= LANES - 2, lanes - LANES, lanes)
    valid = knots < count + 2
    cells = np.arange(4 * count)
    table = spline((cells[:, None] - 4.0 * knots[None, :] - 1.5) / 4.0) * valid[None, :]
    high, low = halves(table)
    gap = count + 8
    forward = (
        high.T.astype(np.float32)
        + np.roll(high.T.astype(np.float32), gap, 0)
        + np.roll(low.T.astype(np.float32), 2 * gap, 0)
    ).astype(bf16)
    return forward, high, low


def area_table(lat_total):
    index = np.arange(lat_total, dtype=np.float32)
    degrees = np.float32(90.0) - (index + np.float32(0.5)) * np.float32(180.0) / np.float32(lat_total)
    values = np.cos((degrees * np.float32(np.pi / 180.0)).astype(np.float64)).astype(np.float32)
    return np.ascontiguousarray(np.broadcast_to(values[:, None], (lat_total, LANES)))


def time_taps():
    taps = []
    for phase in range(4):
        row = []
        for shift in range(-2, 3):
            weight = float(spline((phase - 4.0 * shift - 1.5) / 4.0))
            if weight != 0.0:
                row.append((shift + 2, weight))
        taps.append(row)
    return taps


def split(values):
    high = values.astype(bf16)
    return high, (values - high.astype(f32)).astype(bf16)


def kernel(
    counts,
    mesh_sizes,
    coef_ref,
    inv_ref,
    area_hbm,
    offset_hbm,
    precip_hbm,
    lon_fwd,
    lat_fwd,
    lat_back,
    lon_high,
    lon_low,
    step_ref,
    resid_ref,
    weight,
    precip,
    area,
    cells,
    coef,
    inv,
    res,
    dir0,
    dir1,
    img0,
    img1,
    lon_send,
    lon_recv,
    lat_send,
    lat_recv,
    diag_recv,
    tm_send,
    tm_recv,
    sum_lon,
    sum_lat,
    sum_tm,
    load_sem,
    lon_sems,
    lat_sems,
    diag_sems,
    tm_sems,
    sum_lon_sems,
    sum_lat_sems,
    sum_tm_sems,
):
    time_n, lat_n, lon_n = counts
    padded_time = time_n + 4
    rows = lat_n + 2 * LEAD
    half = LANES // 2
    own_t = slice(2, 2 + time_n)
    own_a = slice(LEAD, LEAD + lat_n)
    me = {name: lax.axis_index(name) for name in AXES}
    size = dict(zip(AXES, mesh_sizes))
    pending = []

    lat_cells = 4 * lat_n
    loads = [
        pltpu.make_async_copy(
            area_hbm.at[pl.ds(pl.multiple_of(me["lat"] * lat_cells, lat_cells), lat_cells)],
            area,
            load_sem.at[0],
        )
    ]
    part = 2 * time_n
    for i in range(2):
        span = pl.ds(i * part, part)
        loads.append(pltpu.make_async_copy(offset_hbm.at[span], weight.at[span], load_sem.at[1 + 2 * i]))
        loads.append(pltpu.make_async_copy(precip_hbm.at[span], precip.at[span], load_sem.at[2 + 2 * i]))
    for load in loads:
        load.start()

    barrier = pltpu.get_barrier_semaphore()
    for name in AXES:
        for hop in range(1, size[name]):
            pl.semaphore_signal(
                barrier,
                inc=1,
                device_id={name: lax.rem(me[name] + hop, size[name])},
                device_id_type=pl.DeviceIdType.MESH,
            )
    for hop in (1, size["lon"] - 1):
        for rise in (1, size["lat"] - 1):
            pl.semaphore_signal(
                barrier,
                inc=1,
                device_id={
                    "lon": lax.rem(me["lon"] + hop, size["lon"]),
                    "lat": lax.rem(me["lat"] + rise, size["lat"]),
                },
                device_id_type=pl.DeviceIdType.MESH,
            )

    coef[...] = jnp.zeros(coef.shape, f32)
    inv[...] = jnp.zeros(inv.shape, f32)
    lane = lax.broadcasted_iota(jnp.int32, (rows, LANES), 1)
    low_lanes = (lane < 2) | (lane >= LANES - 2)
    high_lanes = (lane >= lon_n - 2) & (lane < lon_n + 2)
    used_lanes = (lane < lon_n + 2) | (lane >= LANES - 2)
    own_lanes = lane[0:lat_n] < lon_n
    strip = lax.broadcasted_iota(jnp.int32, (4 * padded_time, LANES), 1)
    batch = LANES // lon_n

    for source, held in ((coef_ref, coef), (inv_ref, inv)):
        for first in range(0, time_n, batch):
            block = source[first : first + batch].reshape(LANES, lat_n)
            if lat_n < LANES:
                block = jnp.concatenate([block, jnp.zeros((LANES, LANES - lat_n), f32)], axis=1)
            turned = block.T[0:lat_n]
            for i in range(batch):
                slab = pltpu.roll(turned, LANES - lon_n * i, 1) if i else turned
                held[2 + first + i, own_a] = jnp.where(own_lanes, slab, 0.0)
    pl.semaphore_wait(barrier, 4 + sum(size[name] - 1 for name in AXES))

    def remote(src, dst, sems, at, name, to):
        return pltpu.make_async_remote_copy(
            src_ref=src,
            dst_ref=dst,
            send_sem=sems.at[0, at],
            recv_sem=sems.at[1, at],
            device_id=to if isinstance(to, dict) else {name: to},
            device_id_type=pl.DeviceIdType.MESH,
        )

    def neighbours(name):
        count = size[name]
        return lax.rem(me[name] + count - 1, count), lax.rem(me[name] + 1, count)

    def exchange(pairs, hooks):
        copies = []
        corners = []
        has_lat = (me["lat"] > 0, me["lat"] < size["lat"] - 1)
        before, after = neighbours("lon")

        def ends(name, send, recv, sems, load, store):
            before, after = neighbours(name)
            has_low = me[name] > 0
            has_high = me[name] < size[name] - 1
            copies = []
            for ref, bank in pairs:
                load(ref, bank)
                down = remote(send.at[bank, 0], recv.at[bank, 1], sems, 2 * bank, name, before)
                up = remote(send.at[bank, 1], recv.at[bank, 0], sems, 2 * bank + 1, name, after)
                pl.when(has_low)(down.start)
                pl.when(has_high)(up.start)
                copies.append((down, up))
                pending.append((has_low, down))
                pending.append((has_high, up))

            def finish():
                for (ref, bank), (down, up) in zip(pairs, copies):

                    @pl.when(has_low)
                    def _():
                        up.wait_recv()
                        store(ref, bank, 0)

                    @pl.when(has_high)
                    def _():
                        down.wait_recv()
                        store(ref, bank, 1)

            return finish

        starts = (LEAD - 2, LEAD + lat_n - 2)

        def lat_load(ref, bank):
            for t in range(padded_time):
                for side, start in enumerate(starts):
                    lat_send[bank, side, 4 * t : 4 * t + 4] = ref[t, start : start + 4]

        def lat_store(ref, bank, side):
            start = starts[side]
            for t in range(padded_time):
                ref[t, start : start + 4] = (
                    ref[t, start : start + 4] + lat_recv[bank, side, 4 * t : 4 * t + 4]
                )

        for ref, bank in pairs:
            packed = jnp.zeros((rows, LANES), f32)
            for t in range(padded_time):
                slab = ref[t]
                at = 4 * t
                packed = jnp.where(
                    (lane >= at) & (lane < at + 4), pltpu.roll(slab, (at + 2) % LANES, 1), packed
                )
                at = half + 4 * t
                packed = jnp.where(
                    (lane >= at) & (lane < at + 4),
                    pltpu.roll(slab, (at - lon_n + 2) % LANES, 1),
                    packed,
                )
            full = jnp.concatenate([packed, jnp.zeros((LANES - rows, LANES), f32)], axis=0)
            lon_send[bank] = full.T
            low = pl.ds(0, 4 * padded_time)
            high = pl.ds(half, 4 * padded_time)
            down = remote(
                lon_send.at[bank, low], lon_recv.at[bank, high], lon_sems, 2 * bank, "lon", before
            )
            up = remote(
                lon_send.at[bank, high], lon_recv.at[bank, low], lon_sems, 2 * bank + 1, "lon", after
            )
            down.start()
            up.start()
            copies.append((down, up))
            pending.append((None, down))
            pending.append((None, up))
            lats = neighbours("lat")
            corner = {}
            for side, (span, to) in enumerate(((low, before), (high, after))):
                for rise in range(2):
                    copy = remote(
                        lon_send.at[bank, span],
                        diag_recv.at[bank, 1 - side, 1 - rise],
                        diag_sems,
                        4 * bank + 2 * side + rise,
                        "lat",
                        {"lon": to, "lat": lats[rise]},
                    )
                    pl.when(has_lat[rise])(copy.start)
                    pending.append((has_lat[rise], copy))
                    corner[1 - side, 1 - rise] = copy
            corners.append(corner)
        finish_lat = ends("lat", lat_send, lat_recv, lat_sems, lat_load, lat_store)
        hooks[0]()
        for (ref, bank), (down, up), corner in zip(pairs, copies, corners):
            down.wait_recv()
            up.wait_recv()
            for rise in range(2):

                @pl.when(has_lat[rise])
                def _():
                    start = LEAD - 2 + rise * lat_n
                    turn = lat_n if rise else LANES - lat_n
                    for side, span in enumerate((low, high)):
                        corner[side, rise].wait_recv()
                        got = pltpu.roll(diag_recv[bank, side, rise], turn % LANES, 1)
                        got = jnp.where((strip >= start) & (strip < start + 4), got, 0.0)
                        lon_recv[bank, span] = lon_recv[bank, span] + got

            back = lon_recv[bank].T[0:rows]
            for t in range(padded_time):
                at = 4 * t
                mine = jnp.where(low_lanes, pltpu.roll(back, (LANES - at - 2) % LANES, 1), 0.0)
                at = half + 4 * t
                mine = jnp.where(high_lanes, pltpu.roll(back, (LANES - at + lon_n - 2) % LANES, 1), mine)
                ref[t] = ref[t] + mine

        finish_lat()

        def tm_load(ref, bank):
            for side, start in enumerate((0, time_n)):
                for i in range(2):
                    tm_send[bank, side, i] = ref[start + 2 * i] + pltpu.roll(
                        ref[start + 2 * i + 1], half, 1
                    )

        def tm_store(ref, bank, side):
            start = (0, time_n)[side]
            for i in range(2):
                got = tm_recv[bank, side, i]
                ref[start + 2 * i] = ref[start + 2 * i] + jnp.where(used_lanes, got, 0.0)
                ref[start + 2 * i + 1] = ref[start + 2 * i + 1] + jnp.where(
                    used_lanes, pltpu.roll(got, half, 1), 0.0
                )

        finish_tm = ends("tm", tm_send, tm_recv, tm_sems, tm_load, tm_store)
        hooks[1]()
        finish_tm()
        hooks[2]()

    slots = {"lon": sum_lon, "lat": sum_lat, "tm": sum_tm}
    slot_sems = {"lon": sum_lon_sems, "lat": sum_lat_sems, "tm": sum_tm_sems}

    class Total:
        def __init__(self, bank, value):
            self.bank, self.value, self.stage = bank, value, 0
            self.send()

        def send(self):
            name = AXES[self.stage]
            count = size[name]
            buf = slots[name]
            buf[self.bank, me[name]] = self.value
            self.copies = []
            for hop in range(1, count):
                at = self.bank * count + hop
                mine = buf.at[self.bank, me[name]]
                out = remote(mine, mine, slot_sems[name], at, name, lax.rem(me[name] + hop, count))
                out.start()
                pending.append((None, out))
                theirs = buf.at[self.bank, lax.rem(me[name] + count - hop, count)]
                self.copies.append(
                    remote(theirs, theirs, slot_sems[name], at, name, lax.rem(me[name] + hop, count))
                )

        def advance(self):
            name = AXES[self.stage]
            for copy in self.copies:
                copy.wait_recv()
            value = slots[name][self.bank, 0]
            for i in range(1, size[name]):
                value = value + slots[name][self.bank, i]
            self.value = value
            self.stage += 1
            if self.stage < len(AXES):
                self.send()

        def read(self, first):
            tile = self.value[8 * first : 8 * first + 8]
            return jnp.sum(jnp.sum(tile, axis=0, keepdims=True), axis=1, keepdims=True)

    def tile_of(values):
        return jnp.sum(values.reshape(-1, 8, LANES), axis=0)

    def own_tile(left, right):
        masked = jnp.where(own_lanes[None], left[own_t, own_a] * right[own_t, own_a], 0.0)
        return tile_of(masked)

    taps = time_taps()

    def synth(z, m, phase):
        total = None
        for at, factor in taps[phase]:
            term = z[m + at] * factor
            total = term if total is None else total + term
        return total

    def columns(t):
        return slice(LANES * t, LANES * (t + 1))

    def apply(vec, image, cell_values, hooks):
        gap = lon_n + 8
        for pair in range(padded_time // 2):
            values = vec[2 * pair : 2 * pair + 2].reshape(2 * rows, LANES)
            high = values.astype(bf16).astype(f32)
            low = values - high
            stacked = (high + pltpu.roll(low, gap, 1) + pltpu.roll(high, 2 * gap, 1)).astype(bf16)
            wide = jnp.dot(stacked, lon_fwd[...], preferred_element_type=f32)
            high, low = split(jnp.concatenate([wide[0:rows], wide[rows:]], axis=1))
            stacked = jnp.concatenate([high, low, high], axis=0)
            cells[:, 2 * LANES * pair : 2 * LANES * (pair + 1)] = jnp.dot(
                lat_fwd[...], stacked, preferred_element_type=f32
            )
        hooks[0]()

        def group(g, carry):
            at = pl.ds(pl.multiple_of(g * 8, 8), 8)
            z = [cells[at, columns(t)] for t in range(padded_time)]
            sums = [None] * padded_time
            for m in range(time_n):
                for phase in range(4):
                    value = cell_values(4 * m + phase, at, synth(z, m, phase))
                    for shift, factor in taps[phase]:
                        term = value * factor
                        old = sums[m + shift]
                        sums[m + shift] = term if old is None else old + term
                cells[at, columns(m)] = sums[m]
            for t in range(time_n, padded_time):
                cells[at, columns(t)] = sums[t]
            return carry

        lax.fori_loop(0, lat_cells // 8, group, 0)
        hooks[1]()
        for pair in range(padded_time // 2):
            high, low = split(cells[:, 2 * LANES * pair : 2 * LANES * (pair + 1)])
            both = jnp.dot(lat_back[...], high, preferred_element_type=f32)
            rest = jnp.dot(lat_back[0:rows], low, preferred_element_type=f32)
            knots = both[0:rows] + both[rows:] + rest
            high, low = split(jnp.concatenate([knots[:, 0:LANES], knots[:, LANES:]], axis=0))
            out = (
                jnp.dot(high, lon_high[...], preferred_element_type=f32)
                + jnp.dot(low, lon_high[...], preferred_element_type=f32)
                + jnp.dot(high, lon_low[...], preferred_element_type=f32)
            )
            image[2 * pair] = out[0:rows]
            image[2 * pair + 1] = out[rows:]
        for t in range(2, 2 + time_n):
            mid = vec[t, own_a]
            outer = vec[t - 2, own_a] + vec[t + 2, own_a]
            inner = vec[t - 1, own_a] + vec[t + 1, own_a]
            outer = outer + vec[t, LEAD - 2 : LEAD + lat_n - 2] + vec[t, LEAD + 2 : LEAD + lat_n + 2]
            inner = inner + vec[t, LEAD - 1 : LEAD + lat_n - 1] + vec[t, LEAD + 1 : LEAD + lat_n + 1]
            outer = outer + pltpu.roll(mid, 2, 1) + pltpu.roll(mid, LANES - 2, 1)
            inner = inner + pltpu.roll(mid, 1, 1) + pltpu.roll(mid, LANES - 1, 1)
            bent = smooth * (18.0 * mid - 4.0 * inner + outer)
            image[t, own_a] = image[t, own_a] + jnp.where(own_lanes, bent, 0.0)
        hooks[2]()

    def nothing():
        pass

    idle = (nothing, nothing, nothing)

    def gradient_cells(s, at, value):
        linear = weight[s, at] + value
        scale = area[at]
        rate = scale * jnp.exp((2.0 - tweedie_power) * linear)
        tilted = scale * jnp.exp((1.0 - tweedie_power) * linear)
        weight[s, at] = rate
        return rate - precip[s, at] * tilted

    def weighted_cells(s, at, value):
        return weight[s, at] * value

    exchange(((coef, 0), (inv, 1)), idle)
    for load in loads:
        load.wait()
    apply(coef, img0, gradient_cells, idle)
    exchange(((img0, 2),), idle)
    res[...] = -img0[...]
    dir0[...] = inv[...] * res[...]
    first_norm = own_tile(res, dir0)

    apply(dir0, img0, weighted_cells, idle)
    sums = Total(0, jnp.concatenate([first_norm, tile_of(dir0[...] * img0[...])], axis=0))
    exchange(((img0, 3),), (sums.advance,) * 3)
    norm = sums.read(0)
    first_step = norm / sums.read(1)
    res[...] = res[...] - first_step[None] * img0[...]
    dir1[...] = inv[...] * res[...]
    tile = own_tile(res, dir1)
    sums = Total(1, jnp.concatenate([tile, jnp.zeros_like(tile)], axis=0))

    apply(dir1, img1, weighted_cells, (sums.advance,) * 3)
    next_norm = sums.read(0)
    beta = next_norm / norm
    dir1[...] = dir1[...] + beta[None] * dir0[...]
    tile = tile_of(dir1[...] * img1[...]) + beta * own_tile(dir1, img0)
    sums = Total(2, jnp.concatenate([tile, jnp.zeros_like(tile)], axis=0))
    exchange(((img1, 4),), (sums.advance,) * 3)
    second_step = next_norm / sums.read(0)
    for first in range(0, time_n, batch):
        packed = [None, None]
        for i in range(batch):
            at = (first + i + 2, own_a)
            step = first_step * dir0[at] + second_step * dir1[at]
            left = res[at] - second_step * (img1[at] + beta * img0[at])
            for which, value in enumerate((step, left)):
                slab = jnp.where(own_lanes, value, 0.0)
                slab = pltpu.roll(slab, lon_n * i, 1) if i else slab
                packed[which] = slab if i == 0 else packed[which] + slab
        for ref, value in zip((step_ref, resid_ref), packed):
            if lat_n < LANES:
                value = jnp.concatenate([value, jnp.zeros((LANES - lat_n, LANES), f32)], axis=0)
            ref[first : first + batch] = value.T[:, 0:lat_n].reshape(batch, lon_n, lat_n)
    for condition, copy in pending:
        if condition is None:
            copy.wait_send()
        else:
            pl.when(condition)(copy.wait_send)


def hand_on(step_ref, resid_ref, step_out, resid_out):
    step_out[...] = step_ref[...]
    resid_out[...] = resid_ref[...]


def solution(mesh):
    mesh_sizes = tuple(mesh.shape[name] for name in AXES)

    def per_device(precip, offset, coefficients, inverse_diag):
        time_n, lat_n, lon_n = coefficients.shape
        hours, lat_cells, lon_cells = precip.shape
        assert lon_cells == LANES and 3 * (lon_n + 8) <= LANES and 8 * (time_n + 4) <= LANES
        assert LANES % lon_n == 0 and time_n % (LANES // lon_n) == 0 and lat_n <= LANES
        rows = lat_n + 2 * LEAD
        padded_time = time_n + 4
        lat_fwd, lat_back = lat_tables(lat_n)
        lon_fwd, lon_high, lon_low = lon_tables(lon_n)
        knots = pltpu.VMEM((padded_time, rows, LANES), f32)
        n_lon, n_lat, n_tm = mesh_sizes
        banks, totals = 5, 3
        vmem = pl.BlockSpec(memory_space=pltpu.VMEM)
        hbm = pl.BlockSpec(memory_space=pl.ANY)
        shape = jax.ShapeDtypeStruct((time_n, lon_n, lat_n), f32)
        dma = pltpu.SemaphoreType.DMA
        step, left = pl.pallas_call(
            functools.partial(kernel, (time_n, lat_n, lon_n), mesh_sizes),
            out_shape=(shape, shape),
            in_specs=[vmem, vmem, hbm, hbm, hbm] + [vmem] * 5,
            out_specs=(vmem, vmem),
            scratch_shapes=[
                pltpu.VMEM((hours, lat_cells, lon_cells), f32),
                pltpu.VMEM((hours, lat_cells, lon_cells), f32),
                pltpu.VMEM((lat_cells, LANES), f32),
                pltpu.VMEM((lat_cells, padded_time * LANES), f32),
            ]
            + [knots] * 7
            + [
                pltpu.VMEM((banks, LANES, LANES), f32),
                pltpu.VMEM((banks, LANES, LANES), f32),
                pltpu.VMEM((banks, 2, 4 * padded_time, LANES), f32),
                pltpu.VMEM((banks, 2, 4 * padded_time, LANES), f32),
                pltpu.VMEM((banks, 2, 2, 4 * padded_time, LANES), f32),
                pltpu.VMEM((banks, 2, 2, rows, LANES), f32),
                pltpu.VMEM((banks, 2, 2, rows, LANES), f32),
                pltpu.VMEM((totals, n_lon, 16, LANES), f32),
                pltpu.VMEM((totals, n_lat, 16, LANES), f32),
                pltpu.VMEM((totals, n_tm, 16, LANES), f32),
                dma((5,)),
                dma((2, 2 * banks)),
                dma((2, 2 * banks)),
                dma((2, 4 * banks)),
                dma((2, 2 * banks)),
                dma((2, totals * n_lon)),
                dma((2, totals * n_lat)),
                dma((2, totals * n_tm)),
            ],
            compiler_params=pltpu.CompilerParams(
                collective_id=0, has_side_effects=True, vmem_limit_bytes=60 * 1024 * 1024
            ),
        )(
            jnp.swapaxes(coefficients, 1, 2),
            jnp.swapaxes(inverse_diag, 1, 2),
            jnp.asarray(area_table(lat_cells * n_lat)),
            offset,
            precip,
            jnp.asarray(lon_fwd),
            jnp.asarray(lat_fwd),
            jnp.asarray(lat_back),
            jnp.asarray(lon_high),
            jnp.asarray(lon_low),
        )
        step, left = pl.pallas_call(
            hand_on, out_shape=(shape, shape), in_specs=[vmem, vmem], out_specs=(vmem, vmem)
        )(step, left)
        return jnp.swapaxes(step, 1, 2), jnp.swapaxes(left, 1, 2)

    spec = P("tm", "lat", "lon")
    return jax.shard_map(
        per_device,
        mesh=mesh,
        in_specs=(spec,) * 4,
        out_specs=(spec,) * 2,
        check_vma=False,
    )
```

```python
import functools

import numpy as np
import jax
import jax.numpy as jnp
from jax import lax
from jax.experimental import pallas as pl
from jax.experimental.pallas import tpu as pltpu
from jax.sharding import PartitionSpec as P

tweedie_power = 1.6
smooth = 0.5
bf16 = jnp.bfloat16
f32 = jnp.float32
LANES = 128
LEAD = 8
AXES = ("lon", "lat", "tm")


def spline(offsets):
    distance = np.abs(np.asarray(offsets, np.float64))
    near_part = (4.0 - 6.0 * distance**2 + 3.0 * distance**3) / 6.0
    far_part = np.maximum(2.0 - distance, 0.0) ** 3 / 6.0
    return np.where(distance < 1.0, near_part, far_part)


def halves(table):
    high = table.astype(np.float32).astype(bf16)
    low = (table - high.astype(np.float64)).astype(np.float32).astype(bf16)
    return high, low


def lat_tables(count):
    knots = np.arange(count + 2 * LEAD) - LEAD
    cells = np.arange(4 * count)
    high, low = halves(
        float(spline(0.125)) * spline((cells[:, None] - 4.0 * knots[None, :] - 1.5) / 4.0)
    )
    forward = np.concatenate([high, high, low], axis=1)
    back = np.concatenate([high.T, low.T], axis=0)
    return forward, back


def lon_tables(count):
    lanes = np.arange(LANES)
    knots = np.where(lanes >= LANES - 2, lanes - LANES, lanes)
    valid = knots < count + 2
    cells = np.arange(4 * count)
    table = spline((cells[:, None] - 4.0 * knots[None, :] - 1.5) / 4.0) * valid[None, :]
    high, low = halves(table)
    gap = count + 8
    forward = (
        high.T.astype(np.float32)
        + np.roll(high.T.astype(np.float32), gap, 0)
        + np.roll(low.T.astype(np.float32), 2 * gap, 0)
    ).astype(bf16)
    return forward, high, low


def area_table(lat_total):
    index = np.arange(lat_total, dtype=np.float32)
    degrees = np.float32(90.0) - (index + np.float32(0.5)) * np.float32(180.0) / np.float32(lat_total)
    values = np.cos((degrees * np.float32(np.pi / 180.0)).astype(np.float64)).astype(np.float32)
    return np.ascontiguousarray(np.broadcast_to(values[:, None], (lat_total, LANES)))


def time_taps():
    taps = []
    for phase in range(4):
        row = []
        for shift in range(-2, 3):
            weight = float(spline((phase - 4.0 * shift - 1.5) / 4.0) / spline(0.125))
            if weight != 0.0:
                row.append((shift + 2, weight))
        taps.append(row)
    return taps


def split(values):
    high = values.astype(bf16)
    return high, (values - high.astype(f32)).astype(bf16)


def kernel(
    counts,
    mesh_sizes,
    coef_ref,
    inv_ref,
    area_hbm,
    offset_hbm,
    precip_hbm,
    lon_fwd,
    lat_fwd,
    lat_back,
    lon_high,
    lon_low,
    step_ref,
    resid_ref,
    weight,
    precip,
    area,
    cells,
    coef,
    inv,
    res,
    dir0,
    dir1,
    img0,
    img1,
    lon_send,
    lon_recv,
    lat_send,
    lat_recv,
    tm_send,
    tm_recv,
    sum_lon,
    sum_lat,
    sum_tm,
    load_sem,
    lon_sems,
    lat_sems,
    tm_sems,
    sum_lon_sems,
    sum_lat_sems,
    sum_tm_sems,
):
    time_n, lat_n, lon_n = counts
    padded_time = time_n + 4
    rows = lat_n + 2 * LEAD
    half = LANES // 2
    own_t = slice(2, 2 + time_n)
    own_a = slice(LEAD, LEAD + lat_n)
    me = {name: lax.axis_index(name) for name in AXES}
    size = dict(zip(AXES, mesh_sizes))
    pending = []

    lat_cells = 4 * lat_n
    loads = [
        pltpu.make_async_copy(
            area_hbm.at[pl.ds(pl.multiple_of(me["lat"] * lat_cells, lat_cells), lat_cells)],
            area,
            load_sem.at[0],
        )
    ]
    part = 2 * time_n
    for i in range(2):
        span = pl.ds(i * part, part)
        loads.append(pltpu.make_async_copy(offset_hbm.at[span], weight.at[span], load_sem.at[1 + 2 * i]))
        loads.append(pltpu.make_async_copy(precip_hbm.at[span], precip.at[span], load_sem.at[2 + 2 * i]))
    for load in loads:
        load.start()

    barrier = pltpu.get_barrier_semaphore()
    for name in AXES:
        for hop in range(1, size[name]):
            pl.semaphore_signal(
                barrier,
                inc=1,
                device_id={name: lax.rem(me[name] + hop, size[name])},
                device_id_type=pl.DeviceIdType.MESH,
            )

    coef[...] = jnp.zeros(coef.shape, f32)
    inv[...] = jnp.zeros(inv.shape, f32)
    lane = lax.broadcasted_iota(jnp.int32, (rows, LANES), 1)
    low_lanes = (lane < 2) | (lane >= LANES - 2)
    high_lanes = (lane >= lon_n - 2) & (lane < lon_n + 2)
    used_lanes = (lane < lon_n + 2) | (lane >= LANES - 2)
    own_lanes = lane[0:lat_n] < lon_n
    batch = LANES // lon_n

    for source, held in ((coef_ref, coef), (inv_ref, inv)):
        for first in range(0, time_n, batch):
            block = source[first : first + batch].reshape(LANES, lat_n)
            if lat_n < LANES:
                block = jnp.concatenate([block, jnp.zeros((LANES, LANES - lat_n), f32)], axis=1)
            turned = block.T[0:lat_n]
            for i in range(batch):
                slab = pltpu.roll(turned, LANES - lon_n * i, 1) if i else turned
                held[2 + first + i, own_a] = jnp.where(own_lanes, slab, 0.0)
    pl.semaphore_wait(barrier, sum(size[name] - 1 for name in AXES))

    def remote(src, dst, sems, at, name, to):
        return pltpu.make_async_remote_copy(
            src_ref=src,
            dst_ref=dst,
            send_sem=sems.at[0, at],
            recv_sem=sems.at[1, at],
            device_id={name: to},
            device_id_type=pl.DeviceIdType.MESH,
        )

    def neighbours(name):
        count = size[name]
        return lax.rem(me[name] + count - 1, count), lax.rem(me[name] + 1, count)

    def exchange(pairs, hooks):
        copies = []
        before, after = neighbours("lon")
        for ref, bank in pairs:
            packed = jnp.zeros((rows, LANES), f32)
            for t in range(padded_time):
                slab = ref[t]
                at = 4 * t
                packed = jnp.where(
                    (lane >= at) & (lane < at + 4), pltpu.roll(slab, (at + 2) % LANES, 1), packed
                )
                at = half + 4 * t
                packed = jnp.where(
                    (lane >= at) & (lane < at + 4),
                    pltpu.roll(slab, (at - lon_n + 2) % LANES, 1),
                    packed,
                )
            full = jnp.concatenate([packed, jnp.zeros((LANES - rows, LANES), f32)], axis=0)
            lon_send[bank] = full.T
            low = pl.ds(0, 4 * padded_time)
            high = pl.ds(half, 4 * padded_time)
            down = remote(
                lon_send.at[bank, low], lon_recv.at[bank, high], lon_sems, 2 * bank, "lon", before
            )
            up = remote(
                lon_send.at[bank, high], lon_recv.at[bank, low], lon_sems, 2 * bank + 1, "lon", after
            )
            down.start()
            up.start()
            copies.append((down, up))
            pending.append((None, down))
            pending.append((None, up))
        hooks[0]()
        for (ref, bank), (down, up) in zip(pairs, copies):
            down.wait_recv()
            up.wait_recv()
            back = lon_recv[bank].T[0:rows]
            for t in range(padded_time):
                at = 4 * t
                mine = jnp.where(low_lanes, pltpu.roll(back, (LANES - at - 2) % LANES, 1), 0.0)
                at = half + 4 * t
                mine = jnp.where(high_lanes, pltpu.roll(back, (LANES - at + lon_n - 2) % LANES, 1), mine)
                ref[t] = ref[t] + mine

        def ends(name, send, recv, sems, load, store, hook):
            before, after = neighbours(name)
            has_low = me[name] > 0
            has_high = me[name] < size[name] - 1
            copies = []
            for ref, bank in pairs:
                load(ref, bank)
                down = remote(send.at[bank, 0], recv.at[bank, 1], sems, 2 * bank, name, before)
                up = remote(send.at[bank, 1], recv.at[bank, 0], sems, 2 * bank + 1, name, after)
                pl.when(has_low)(down.start)
                pl.when(has_high)(up.start)
                copies.append((down, up))
                pending.append((has_low, down))
                pending.append((has_high, up))
            hook()
            for (ref, bank), (down, up) in zip(pairs, copies):

                @pl.when(has_low)
                def _():
                    up.wait_recv()
                    store(ref, bank, 0)

                @pl.when(has_high)
                def _():
                    down.wait_recv()
                    store(ref, bank, 1)

        starts = (LEAD - 2, LEAD + lat_n - 2)

        def lat_load(ref, bank):
            for t in range(padded_time):
                for side, start in enumerate(starts):
                    lat_send[bank, side, 4 * t : 4 * t + 4] = ref[t, start : start + 4]

        def lat_store(ref, bank, side):
            start = starts[side]
            for t in range(padded_time):
                ref[t, start : start + 4] = (
                    ref[t, start : start + 4] + lat_recv[bank, side, 4 * t : 4 * t + 4]
                )

        ends("lat", lat_send, lat_recv, lat_sems, lat_load, lat_store, hooks[1])

        def tm_load(ref, bank):
            for side, start in enumerate((0, time_n)):
                for i in range(2):
                    tm_send[bank, side, i] = ref[start + 2 * i] + pltpu.roll(
                        ref[start + 2 * i + 1], half, 1
                    )

        def tm_store(ref, bank, side):
            start = (0, time_n)[side]
            for i in range(2):
                got = tm_recv[bank, side, i]
                ref[start + 2 * i] = ref[start + 2 * i] + jnp.where(used_lanes, got, 0.0)
                ref[start + 2 * i + 1] = ref[start + 2 * i + 1] + jnp.where(
                    used_lanes, pltpu.roll(got, half, 1), 0.0
                )

        ends("tm", tm_send, tm_recv, tm_sems, tm_load, tm_store, hooks[2])

    slots = {"lon": sum_lon, "lat": sum_lat, "tm": sum_tm}
    slot_sems = {"lon": sum_lon_sems, "lat": sum_lat_sems, "tm": sum_tm_sems}

    class Total:
        def __init__(self, bank, value):
            self.bank, self.value, self.stage = bank, value, 0
            self.send()

        def send(self):
            name = AXES[self.stage]
            count = size[name]
            buf = slots[name]
            buf[self.bank, me[name]] = self.value
            self.copies = []
            for hop in range(1, count):
                at = self.bank * count + hop
                mine = buf.at[self.bank, me[name]]
                out = remote(mine, mine, slot_sems[name], at, name, lax.rem(me[name] + hop, count))
                out.start()
                pending.append((None, out))
                theirs = buf.at[self.bank, lax.rem(me[name] + count - hop, count)]
                self.copies.append(
                    remote(theirs, theirs, slot_sems[name], at, name, lax.rem(me[name] + hop, count))
                )

        def advance(self):
            name = AXES[self.stage]
            for copy in self.copies:
                copy.wait_recv()
            value = slots[name][self.bank, 0]
            for i in range(1, size[name]):
                value = value + slots[name][self.bank, i]
            self.value = value
            self.stage += 1
            if self.stage < len(AXES):
                self.send()

        def read(self, first):
            tile = self.value[8 * first : 8 * first + 8]
            return jnp.sum(jnp.sum(tile, axis=0, keepdims=True), axis=1, keepdims=True)

    def tile_of(values):
        return jnp.sum(values.reshape(-1, 8, LANES), axis=0)

    def own_tile(left, right):
        masked = jnp.where(own_lanes[None], left[own_t, own_a] * right[own_t, own_a], 0.0)
        return tile_of(masked)

    taps = time_taps()

    def synth(z, m, phase):
        total = None
        for at, factor in taps[phase]:
            term = z[m + at] if factor == 1.0 else z[m + at] * factor
            total = term if total is None else total + term
        return total

    def columns(t):
        return slice(LANES * t, LANES * (t + 1))

    def apply(vec, image, cell_values, hooks):
        gap = lon_n + 8
        for pair in range(padded_time // 2):
            values = vec[2 * pair : 2 * pair + 2].reshape(2 * rows, LANES)
            high = values.astype(bf16).astype(f32)
            low = values - high
            stacked = (high + pltpu.roll(low, gap, 1) + pltpu.roll(high, 2 * gap, 1)).astype(bf16)
            wide = jnp.dot(stacked, lon_fwd[...], preferred_element_type=f32)
            high, low = split(jnp.concatenate([wide[0:rows], wide[rows:]], axis=1))
            stacked = jnp.concatenate([high, low, high], axis=0)
            cells[:, 2 * LANES * pair : 2 * LANES * (pair + 1)] = jnp.dot(
                lat_fwd[...], stacked, preferred_element_type=f32
            )
        hooks[0]()

        def group(g, carry):
            at = pl.ds(pl.multiple_of(g * 8, 8), 8)
            z = [cells[at, columns(t)] for t in range(padded_time)]
            sums = [None] * padded_time
            for m in range(time_n):
                values = [cell_values(4 * m + phase, at, synth(z, m, phase)) for phase in range(4)]
                terms = [(2, values[1] + values[2]), (2, (values[0] + values[3]) * dict(taps[0])[2])]
                for phase in range(4):
                    for shift, factor in taps[phase]:
                        if shift != 2:
                            terms.append((shift, values[phase] * factor))
                for shift, term in terms:
                    old = sums[m + shift]
                    sums[m + shift] = term if old is None else old + term
                cells[at, columns(m)] = sums[m]
            for t in range(time_n, padded_time):
                cells[at, columns(t)] = sums[t]
            return carry

        lax.fori_loop(0, lat_cells // 8, group, 0)
        hooks[1]()
        for pair in range(padded_time // 2):
            high, low = split(cells[:, 2 * LANES * pair : 2 * LANES * (pair + 1)])
            both = jnp.dot(lat_back[...], high, preferred_element_type=f32)
            rest = jnp.dot(lat_back[0:rows], low, preferred_element_type=f32)
            knots = both[0:rows] + both[rows:] + rest
            high, low = split(jnp.concatenate([knots[:, 0:LANES], knots[:, LANES:]], axis=0))
            out = (
                jnp.dot(high, lon_high[...], preferred_element_type=f32)
                + jnp.dot(low, lon_high[...], preferred_element_type=f32)
                + jnp.dot(high, lon_low[...], preferred_element_type=f32)
            )
            image[2 * pair] = out[0:rows]
            image[2 * pair + 1] = out[rows:]
        for t in range(2, 2 + time_n):
            mid = vec[t, own_a]
            outer = vec[t - 2, own_a] + vec[t + 2, own_a]
            inner = vec[t - 1, own_a] + vec[t + 1, own_a]
            outer = outer + vec[t, LEAD - 2 : LEAD + lat_n - 2] + vec[t, LEAD + 2 : LEAD + lat_n + 2]
            inner = inner + vec[t, LEAD - 1 : LEAD + lat_n - 1] + vec[t, LEAD + 1 : LEAD + lat_n + 1]
            outer = outer + pltpu.roll(mid, 2, 1) + pltpu.roll(mid, LANES - 2, 1)
            inner = inner + pltpu.roll(mid, 1, 1) + pltpu.roll(mid, LANES - 1, 1)
            bent = smooth * (18.0 * mid - 4.0 * inner + outer)
            image[t, own_a] = image[t, own_a] + jnp.where(own_lanes, bent, 0.0)
        hooks[2]()

    def nothing():
        pass

    idle = (nothing, nothing, nothing)

    def gradient_cells(s, at, value):
        linear = weight[s, at] + value
        scale = area[at]
        rate = scale * jnp.exp((2.0 - tweedie_power) * linear)
        tilted = scale * jnp.exp((1.0 - tweedie_power) * linear)
        weight[s, at] = rate
        return rate - precip[s, at] * tilted

    def weighted_cells(s, at, value):
        return weight[s, at] * value

    exchange(((coef, 0), (inv, 1)), idle)
    for load in loads:
        load.wait()
    apply(coef, img0, gradient_cells, idle)
    exchange(((img0, 2),), idle)
    res[...] = -img0[...]
    dir0[...] = inv[...] * res[...]
    first_norm = own_tile(res, dir0)

    apply(dir0, img0, weighted_cells, idle)
    sums = Total(0, jnp.concatenate([first_norm, tile_of(dir0[...] * img0[...])], axis=0))
    exchange(((img0, 3),), (sums.advance,) * 3)
    norm = sums.read(0)
    first_step = norm / sums.read(1)
    res[...] = res[...] - first_step[None] * img0[...]
    dir1[...] = inv[...] * res[...]
    tile = own_tile(res, dir1)
    sums = Total(1, jnp.concatenate([tile, jnp.zeros_like(tile)], axis=0))

    apply(dir1, img1, weighted_cells, (sums.advance,) * 3)
    next_norm = sums.read(0)
    beta = next_norm / norm
    dir1[...] = dir1[...] + beta[None] * dir0[...]
    tile = tile_of(dir1[...] * img1[...]) + beta * own_tile(dir1, img0)
    sums = Total(2, jnp.concatenate([tile, jnp.zeros_like(tile)], axis=0))
    exchange(((img1, 4),), (sums.advance,) * 3)
    second_step = next_norm / sums.read(0)
    for first in range(0, time_n, batch):
        packed = [None, None]
        for i in range(batch):
            at = (first + i + 2, own_a)
            step = first_step * dir0[at] + second_step * dir1[at]
            left = res[at] - second_step * (img1[at] + beta * img0[at])
            for which, value in enumerate((step, left)):
                slab = jnp.where(own_lanes, value, 0.0)
                slab = pltpu.roll(slab, lon_n * i, 1) if i else slab
                packed[which] = slab if i == 0 else packed[which] + slab
        for ref, value in zip((step_ref, resid_ref), packed):
            if lat_n < LANES:
                value = jnp.concatenate([value, jnp.zeros((LANES - lat_n, LANES), f32)], axis=0)
            ref[first : first + batch] = value.T[:, 0:lat_n].reshape(batch, lon_n, lat_n)
    for condition, copy in pending:
        if condition is None:
            copy.wait_send()
        else:
            pl.when(condition)(copy.wait_send)


def hand_on(step_ref, resid_ref, step_out, resid_out):
    step_out[...] = step_ref[...]
    resid_out[...] = resid_ref[...]


def solution(mesh):
    mesh_sizes = tuple(mesh.shape[name] for name in AXES)

    def per_device(precip, offset, coefficients, inverse_diag):
        time_n, lat_n, lon_n = coefficients.shape
        hours, lat_cells, lon_cells = precip.shape
        assert lon_cells == LANES and 3 * (lon_n + 8) <= LANES and 8 * (time_n + 4) <= LANES
        assert LANES % lon_n == 0 and time_n % (LANES // lon_n) == 0 and lat_n <= LANES
        rows = lat_n + 2 * LEAD
        padded_time = time_n + 4
        lat_fwd, lat_back = lat_tables(lat_n)
        lon_fwd, lon_high, lon_low = lon_tables(lon_n)
        knots = pltpu.VMEM((padded_time, rows, LANES), f32)
        n_lon, n_lat, n_tm = mesh_sizes
        banks, totals = 5, 3
        vmem = pl.BlockSpec(memory_space=pltpu.VMEM)
        hbm = pl.BlockSpec(memory_space=pl.ANY)
        shape = jax.ShapeDtypeStruct((time_n, lon_n, lat_n), f32)
        dma = pltpu.SemaphoreType.DMA
        step, left = pl.pallas_call(
            functools.partial(kernel, (time_n, lat_n, lon_n), mesh_sizes),
            out_shape=(shape, shape),
            in_specs=[vmem, vmem, hbm, hbm, hbm] + [vmem] * 5,
            out_specs=(vmem, vmem),
            scratch_shapes=[
                pltpu.VMEM((hours, lat_cells, lon_cells), f32),
                pltpu.VMEM((hours, lat_cells, lon_cells), f32),
                pltpu.VMEM((lat_cells, LANES), f32),
                pltpu.VMEM((lat_cells, padded_time * LANES), f32),
            ]
            + [knots] * 7
            + [
                pltpu.VMEM((banks, LANES, LANES), f32),
                pltpu.VMEM((banks, LANES, LANES), f32),
                pltpu.VMEM((banks, 2, 4 * padded_time, LANES), f32),
                pltpu.VMEM((banks, 2, 4 * padded_time, LANES), f32),
                pltpu.VMEM((banks, 2, 2, rows, LANES), f32),
                pltpu.VMEM((banks, 2, 2, rows, LANES), f32),
                pltpu.VMEM((totals, n_lon, 16, LANES), f32),
                pltpu.VMEM((totals, n_lat, 16, LANES), f32),
                pltpu.VMEM((totals, n_tm, 16, LANES), f32),
                dma((5,)),
                dma((2, 2 * banks)),
                dma((2, 2 * banks)),
                dma((2, 2 * banks)),
                dma((2, totals * n_lon)),
                dma((2, totals * n_lat)),
                dma((2, totals * n_tm)),
            ],
            compiler_params=pltpu.CompilerParams(
                collective_id=0, has_side_effects=True, vmem_limit_bytes=60 * 1024 * 1024
            ),
        )(
            jnp.swapaxes(coefficients, 1, 2),
            jnp.swapaxes(inverse_diag, 1, 2),
            jnp.asarray(area_table(lat_cells * n_lat)),
            offset,
            precip,
            jnp.asarray(lon_fwd),
            jnp.asarray(lat_fwd),
            jnp.asarray(lat_back),
            jnp.asarray(lon_high),
            jnp.asarray(lon_low),
        )
        step, left = pl.pallas_call(
            hand_on, out_shape=(shape, shape), in_specs=[vmem, vmem], out_specs=(vmem, vmem)
        )(step, left)
        return jnp.swapaxes(step, 1, 2), jnp.swapaxes(left, 1, 2)

    spec = P("tm", "lat", "lon")
    return jax.shard_map(
        per_device,
        mesh=mesh,
        in_specs=(spec,) * 4,
        out_specs=(spec,) * 2,
        check_vma=False,
    )
```
